512 devices in a mesh: grp: 16 (over y_hi, x, core), blk: 32 (over z, y_lo).
Axes of the slice: x: 4, y: 8 (y_hi: 2, y_lo: 4; y = y_hi * 4 + y_lo), z: 8, core: 2. Of those that a mesh axis runs over, the one named last changes fastest.
Arguments:
- vertex: float32 [16, 32, 1024, 256], P('grp', 'blk'), may hold values from -1.5 to 1.5
- context: float32 [16, 32, 96, 256], P('grp', 'blk'), may hold values from -1.5 to 1.5
- counts: int32 [16, 32, 6, 96, 1024], P('grp', 'blk'), may hold values from 0 to 7
- tile_index: int32 [16, 32, 6], P('grp', 'blk'), may hold values from 0 to 5, each once within a row
- matching: int32 [16], replicated, may hold values from 0 to 15, as said below
Outputs:
- vertex_out: float32 [16, 32, 1024, 256], P('grp', 'blk')
- context_out: float32 [16, 32, 96, 256], P('grp', 'blk')
The draws below stay inside these ranges and needn't reach their ends.
Inputs may be any that keep to these rules, and one draw needn't show every extreme that they name: matching names every group once. `tile_index`: each row over the last dimension names every stored tile once.
All inputs are finite; a program needn't handle non-finite values.
Results may differ from the reference program's by a relative error of at most 0.00014.
Values sent between devices are 32-bit elements; how exact they have to be, the bound alone decides.
No kernel may reach another device: no remote copies, remote signals or barrier semaphores. Data moves between devices by JAX's collectives and lax.ppermute only.
A program may use at most 64 MiB of HBM per device.

```python
import jax
import jax.numpy as jnp
from jax import lax

D = 256
VR = 1024
CR = 96
STEPS = 6
FIRST = 4
N_GRP = 16
N_BLK = 32


def draw_matching(key, part):
    first_key = jax.random.fold_in(key, 11)
    second_key = jax.random.fold_in(key, 23)
    shuffled = jax.random.permutation(first_key, jnp.arange(N_GRP, dtype=jnp.int32)).astype(jnp.int32)
    source = jax.random.randint(second_key, (), 0, N_GRP, dtype=jnp.int32)
    target = ((source + N_GRP // 2) % N_GRP).astype(jnp.int32)
    holder = jnp.argmax((shuffled == target).astype(jnp.int32)).astype(jnp.int32)
    previous = shuffled[source]
    shuffled = shuffled.at[holder].set(previous)
    shuffled = shuffled.at[source].set(target)
    return shuffled.astype(jnp.int32)


def plant(values, key, low, largest):
    shape = values.shape
    place = [jax.random.randint(jax.random.fold_in(key, axis), (), 0, shape[axis]) for axis in range(len(shape))]
    values = values.at[tuple(place)].set(low)
    longest = shape.index(max(shape))
    place[longest] = (place[longest] + 1) % shape[longest]
    return values.at[tuple(place)].set(largest)


def level_of(own_key, dims, shards, smallest, high):
    loudness, own = 1.0, jax.random.fold_in(own_key, 6)
    for dim, blocks in shards:
        heights = jnp.exp(jax.random.uniform(jax.random.fold_in(own, dim), (blocks,), jnp.float32, smallest / len(shards), high / len(shards)))
        loudness = loudness * jnp.repeat(heights, dims[dim] // blocks).reshape([-1 if axis == dim else 1 for axis in range(len(dims))])
    return loudness


def centred(key, shape, scale, reach, pieces=(), kind=jnp.bfloat16):
    entries = jax.random.normal(key, shape, jnp.float32) * scale
    if len(pieces) > 0:
        entries = level_of(key, shape, pieces, -0.22, 0.18) * entries
    return jnp.clip(entries, min=-reach, max=reach).astype(kind)


def setup_inputs(seed: int = 0) -> dict:
    arg_keys = jax.random.split(jax.random.key(seed), 6)
    return {
        "vertex": centred(arg_keys[0], (N_GRP, N_BLK, VR, D), 0.25, 1.5, ((0, 16), (1, 32)), jnp.float32),
        "context": centred(arg_keys[1], (N_GRP, N_BLK, CR, D), 0.25, 1.5, ((0, 16), (1, 32)), jnp.float32),
        "counts": plant(jax.random.randint(arg_keys[2], (N_GRP, N_BLK, STEPS, CR, VR), 0, 8), jax.random.fold_in(arg_keys[2], 1), 0, 7).astype(jnp.int32),
        "tile_index": jax.vmap(lambda own: jax.random.permutation(own, STEPS))(jax.random.split(arg_keys[3], N_GRP * N_BLK)).reshape((N_GRP, N_BLK, STEPS)).astype(jnp.int32),
        "matching": draw_matching(jax.random.fold_in(arg_keys[5], 71), 0),
    }


lr_rate = 0.003


def update(vertex_rows, context_rows, weight_tile):
    logits = jnp.dot(context_rows, vertex_rows.T, precision=lax.Precision.HIGHEST, preferred_element_type=jnp.float32)
    gradient_logit = (weight_tile + 1.0) * jax.nn.sigmoid(logits) - weight_tile
    vertex_grad = jnp.dot(gradient_logit.T, context_rows, precision=lax.Precision.HIGHEST, preferred_element_type=jnp.float32)
    context_grad = jnp.dot(gradient_logit, vertex_rows, precision=lax.Precision.HIGHEST, preferred_element_type=jnp.float32)
    return vertex_rows - lr_rate * vertex_grad, context_rows - lr_rate * context_grad


def reference(vertex, context, counts, tile_index, matching):
    groups = vertex.shape[0]
    blocks = vertex.shape[1]
    total = groups * blocks
    vertex_all = vertex.reshape(total, VR, D)
    context_all = context.reshape(total, CR, D)
    count_all = counts.reshape(total, STEPS, CR, VR)
    order_all = tile_index.reshape(total, STEPS)
    for step_num in range(STEPS):
        def one_device(items):
            vertex_rows, context_rows, stored, order = items
            picked = lax.dynamic_index_in_dim(stored, order[step_num], 0, keepdims=False)
            return update(vertex_rows, context_rows, picked.astype(jnp.float32))

        vertex_all, context_all = lax.map(one_device, (vertex_all, context_all, count_all, order_all))
        if step_num + 1 < STEPS:
            shaped = context_all.reshape(groups, blocks, CR, D)
            if step_num + 1 == FIRST:
                shaped = jnp.zeros_like(shaped).at[matching].set(shaped)
            else:
                shaped = jnp.roll(shaped, 1, axis=1)
            context_all = shaped.reshape(total, CR, D)
    return vertex_all.reshape(groups, blocks, VR, D), context_all.reshape(groups, blocks, CR, D)
```

```python
import functools

import jax
import jax.numpy as jnp
from jax import lax
from jax.experimental import pallas as pl
from jax.experimental.pallas import tpu as pltpu
from jax.sharding import PartitionSpec as P

STEPS = 6
FIRST = 4
CR, VR, D = 96, 1024, 256
N_X, N_CORE = 4, 2
N_GRP = 16
lr_rate = 0.003

F32, BF16 = jnp.float32, jnp.bfloat16
CHUNK = 256
PARTS = VR // CHUNK
VMEM = pl.BlockSpec(memory_space=pltpu.VMEM)
SMEM = pl.BlockSpec(memory_space=pltpu.SMEM)
HBM = pl.BlockSpec(memory_space=pltpu.HBM)


def array(shape, dtype=F32):
    return jax.ShapeDtypeStruct(shape, dtype)


def call(kernel, name, out_shape, in_specs, out_specs, flops, moved, scratch=()):
    return pl.pallas_call(
        kernel,
        out_shape=out_shape,
        in_specs=in_specs,
        out_specs=out_specs,
        scratch_shapes=scratch,
        name=name,
        cost_estimate=pl.CostEstimate(flops=flops, bytes_accessed=moved, transcendentals=CR * VR),
        compiler_params=pltpu.CompilerParams(vmem_limit_bytes=16 * 1024 * 1024),
    )


def halves(x):
    high = x.astype(BF16)
    return high, (x - high.astype(F32)).astype(BF16)


def product(a, b, a_dim, b_dim):
    return lax.dot_general(a, b, (((a_dim,), (b_dim,)), ((), ())), preferred_element_type=F32)


def logit_gradient(ch, cc, high, low, weight):
    both = product(cc, high, 1, 1)
    logits = both[:CR] + (both[CR:] + product(ch, low, 1, 1))
    weight = weight.astype(F32)
    return (weight + 1.0) * jax.nn.sigmoid(logits) - weight


def context_part(rh, rl, high, low):
    both = product(jnp.concatenate([rh, rl], 0), high, 0 + 1, 0)
    return both[:CR] + (both[CR:] + product(rh, low, 1, 0))


def vertex_part(rh, rl, double, cl):
    return product(jnp.concatenate([rh, rl], 0), double, 0, 0) + product(rh, cl, 0, 0)


def rows_of(part):
    return pl.ds(part * CHUNK, CHUNK)


def first_kernel(order, vertex, context, counts, c_out, r_out, c_in, u_out, tile, sems):
    copies = [
        pltpu.make_async_copy(context.at[0, 0], c_in, sems.at[0]),
        pltpu.make_async_copy(counts.at[0, 0, order[0, 0, 0]], tile, sems.at[1]),
    ]
    for part in range(PARTS):
        rows = rows_of(part)
        copies.append(
            pltpu.make_async_copy(vertex.at[0, 0, rows, :], u_out.at[rows, :], sems.at[2 + part])
        )
    for copy in copies:
        copy.start()
    copies[0].wait()
    copies[1].wait()
    c = c_in[...]
    ch, cl = halves(c)
    cc = jnp.concatenate([ch, cl], 0)
    total = jnp.zeros((CR, D), F32)
    for part in range(PARTS):
        rows = rows_of(part)
        copies[2 + part].wait()
        high, low = halves(u_out[rows, :])
        r = logit_gradient(ch, cc, high, low, tile[:, rows])
        r_out[:, rows] = r
        total = total + context_part(*halves(r), high, low)
    c_out[...] = c - lr_rate * total


def context_kernel(c_in, high_in, low_in, tile, c_out, r_out):
    c = c_in[...]
    ch, cl = halves(c)
    cc = jnp.concatenate([ch, cl], 0)
    total = jnp.zeros((CR, D), F32)
    for part in range(PARTS):
        rows = rows_of(part)
        high, low = high_in[rows, :], low_in[rows, :]
        r = logit_gradient(ch, cc, high, low, tile[:, rows])
        r_out[:, rows] = r
        total = total + context_part(*halves(r), high, low)
    c_out[...] = c - lr_rate * total


def source_group(matching, group):
    source = jnp.int32(0)
    for k in range(N_GRP):
        source = jnp.where(matching[k] == group, jnp.int32(k), source)
    return source


def x_of(group):
    return (group // N_CORE) % N_X


def pack_kernel(matching, own, held, out):
    group = own[0]
    base = group - x_of(group) * N_CORE
    for x in range(N_X):
        source = source_group(matching, base + x * N_CORE)
        out[x] = held[(source // (N_X * N_CORE)) * N_CORE + source % N_CORE]


def received_kernel(matching, own, received, u_in, tile, c_out, r_out, c_in):
    c = received[x_of(source_group(matching, own[0]))]
    c_in[...] = c
    ch, cl = halves(c)
    cc = jnp.concatenate([ch, cl], 0)
    total = jnp.zeros((CR, D), F32)
    for part in range(PARTS):
        rows = rows_of(part)
        high, low = halves(u_in[rows, :])
        r = logit_gradient(ch, cc, high, low, tile[:, rows])
        r_out[:, rows] = r
        total = total + context_part(*halves(r), high, low)
    c_out[...] = c - lr_rate * total


def vertex_kernel(order, u_in, r_in, c_in, counts, u_out, tile, *rest, step):
    *halves_out, sem = rest
    copy = pltpu.make_async_copy(counts.at[0, 0, order[0, 0, step]], tile, sem)
    copy.start()
    ch, cl = halves(c_in[...])
    double = jnp.concatenate([ch, ch], 0)
    for part in range(PARTS):
        rows = rows_of(part)
        u = u_in[rows, :] - lr_rate * vertex_part(*halves(r_in[:, rows]), double, cl)
        u_out[rows, :] = u
        for half_out, half in zip(halves_out, halves(u)):
            half_out[rows, :] = half
    copy.wait()


def last_kernel(u_in, c_ref, high_in, low_in, tile, vertex_out, context_out, u_new, c_new, sems):
    c = c_ref[...]
    ch, cl = halves(c)
    cc = jnp.concatenate([ch, cl], 0)
    double = jnp.concatenate([ch, ch], 0)
    total = jnp.zeros((CR, D), F32)
    copies = []
    for part in range(PARTS):
        rows = rows_of(part)
        high, low = high_in[rows, :], low_in[rows, :]
        rh, rl = halves(logit_gradient(ch, cc, high, low, tile[:, rows]))
        u_new[rows, :] = u_in[rows, :] - lr_rate * vertex_part(rh, rl, double, cl)
        copies.append(
            pltpu.make_async_copy(u_new.at[rows, :], vertex_out.at[0, 0, rows, :], sems.at[part])
        )
        copies[-1].start()
        total = total + context_part(rh, rl, high, low)
    c_new[...] = c - lr_rate * total
    copies.append(pltpu.make_async_copy(c_new, context_out.at[0, 0], sems.at[PARTS]))
    copies[-1].start()
    for copy in copies:
        copy.wait()


MATMUL = 6 * CR * VR * D
BLOCK = 4 * CR * D
GRADIENT = 4 * CR * VR
VERTEX = 4 * VR * D

UPDATED = (array((CR, D)), array((CR, VR)), array((CR, D)))


def first_step(order, vertex, context, counts):
    return call(
        first_kernel,
        "first_step",
        UPDATED + (array((VR, D)),),
        [SMEM, HBM, HBM, HBM],
        (VMEM,) * 4,
        2 * MATMUL,
        2 * VERTEX,
        [pltpu.VMEM((CR, VR), jnp.int32), pltpu.SemaphoreType.DMA((2 + PARTS,))],
    )(order, vertex, context, counts)


def context_step(c, high, low, tile):
    return call(
        context_kernel,
        "context_step",
        UPDATED[:2],
        [VMEM] * 4,
        (VMEM,) * 2,
        2 * MATMUL,
        VERTEX,
    )(c, high, low, tile)


def received_step(matching, own, received, u, tile):
    return call(
        received_kernel,
        "received_step",
        UPDATED,
        [SMEM] * 2 + [VMEM] * 3,
        (VMEM,) * 3,
        2 * MATMUL,
        VERTEX,
    )(matching, own, received, u, tile)


def vertex_step(order, u, r, c, counts, step):
    outs = (array((VR, D)), array((CR, VR), jnp.int32))
    if step != FIRST:
        outs += (array((VR, D), BF16),) * 2
    return call(
        functools.partial(vertex_kernel, step=step),
        "vertex_step",
        outs,
        [SMEM, VMEM, VMEM, VMEM, HBM],
        (VMEM,) * len(outs),
        MATMUL,
        4 * VERTEX,
        [pltpu.SemaphoreType.DMA],
    )(order, u, r, c, counts)


def last_step(u, c, high, low, tile):
    return call(
        last_kernel,
        "last_step",
        (array((1, 1, VR, D)), array((1, 1, CR, D))),
        [VMEM] * 5,
        (HBM, HBM),
        3 * MATMUL,
        2 * VERTEX,
        [
            pltpu.VMEM((VR, D), F32),
            pltpu.VMEM((CR, D), F32),
            pltpu.SemaphoreType.DMA((PARTS + 1,)),
        ],
    )(u, c, high, low, tile)


def pack(matching, own, held):
    return call(
        pack_kernel,
        "pack",
        array((N_X, CR, D)),
        [SMEM, SMEM, VMEM],
        VMEM,
        0,
        8 * BLOCK,
    )(matching, own, held)


def shifted(block):
    devices = lax.axis_size("blk")
    return lax.ppermute(block, "blk", [(i, (i + 1) % devices) for i in range(devices)])


def on_device(vertex, context, counts, tile_index, matching):
    own = lax.axis_index("grp").astype(jnp.int32).reshape(1)
    vertex, context, counts = (
        pltpu.with_memory_space_constraint(x, pltpu.HBM) for x in (vertex, context, counts)
    )
    half = N_X * N_CORE
    columns = [[g, g + 1, g + half, g + half + 1] for g in range(0, half, N_CORE)]
    rings = [[y * half + x * N_CORE + k for x in range(N_X)] for y in range(2) for k in range(N_CORE)]
    c_new, r, c, u = first_step(tile_index, vertex, context, counts)
    for step in range(1, STEPS):
        if step == FIRST:
            held = lax.all_gather(c_new, "grp", axis_index_groups=columns)
            sent = pack(matching, own, held)
            moved = lax.all_to_all(sent, "grp", 0, 0, axis_index_groups=rings, tiled=True)
        else:
            moved = shifted(c_new)
        u, tile, *split = vertex_step(tile_index, u, r, c, counts, step)
        if step == STEPS - 1:
            return last_step(u, moved, *split, tile)
        if step == FIRST:
            c_new, r, c = received_step(matching, own, moved, u, tile)
        else:
            c = moved
            c_new, r = context_step(c, *split, tile)


def solution(mesh):
    in_specs = (
        P("grp", "blk", None, None),
        P("grp", "blk", None, None),
        P("grp", "blk", None, None, None),
        P("grp", "blk", None),
        P(),
    )
    out_specs = (P("grp", "blk", None, None), P("grp", "blk", None, None))
    return jax.shard_map(
        on_device, mesh=mesh, in_specs=in_specs, out_specs=out_specs, check_vma=False
    )
```

```python
import functools

import jax
import jax.numpy as jnp
from jax import lax
from jax.experimental import pallas as pl
from jax.experimental.pallas import tpu as pltpu
from jax.sharding import PartitionSpec as P

STEPS = 6
FIRST = 4
CR, VR, D = 96, 1024, 256
N_X, N_CORE = 4, 2
N_GRP = 16
lr_rate = 0.003

F32, BF16 = jnp.float32, jnp.bfloat16
CHUNK = 256
PARTS = VR // CHUNK
VMEM = pl.BlockSpec(memory_space=pltpu.VMEM)
SMEM = pl.BlockSpec(memory_space=pltpu.SMEM)
HBM = pl.BlockSpec(memory_space=pltpu.HBM)


def array(shape, dtype=F32):
    return jax.ShapeDtypeStruct(shape, dtype)


def call(kernel, out_shape, in_specs, out_specs, flops, moved, scratch=(), aliases=None):
    return pl.pallas_call(
        kernel,
        out_shape=out_shape,
        in_specs=in_specs,
        out_specs=out_specs,
        scratch_shapes=scratch,
        input_output_aliases=aliases or {},
        cost_estimate=pl.CostEstimate(flops=flops, bytes_accessed=moved, transcendentals=CR * VR),
        compiler_params=pltpu.CompilerParams(vmem_limit_bytes=16 * 1024 * 1024),
    )


def halves(x):
    high = x.astype(BF16)
    return high, (x - high.astype(F32)).astype(BF16)


def product(a, b, a_dim, b_dim):
    return lax.dot_general(a, b, (((a_dim,), (b_dim,)), ((), ())), preferred_element_type=F32)


def logit_gradient(ch, cc, high, low, weight):
    both = product(cc, high, 1, 1)
    logits = both[:CR] + (both[CR:] + product(ch, low, 1, 1))
    weight = weight.astype(F32)
    return (weight + 1.0) * jax.nn.sigmoid(logits) - weight


def context_part(rh, rl, high, low):
    both = product(jnp.concatenate([rh, rl], 0), high, 0 + 1, 0)
    return both[:CR] + (both[CR:] + product(rh, low, 1, 0))


def vertex_part(rh, rl, double, cl):
    return product(jnp.concatenate([rh, rl], 0), double, 0, 0) + product(rh, cl, 0, 0)


def rows_of(part):
    return pl.ds(part * CHUNK, CHUNK)


def first_kernel(order, vertex, context, counts, c_out, r_out, c_in, u_out, tile, sems):
    copies = [
        pltpu.make_async_copy(context.at[0, 0], c_in, sems.at[0]),
        pltpu.make_async_copy(counts.at[0, 0, order[0, 0, 0]], tile, sems.at[1]),
    ]
    for part in range(PARTS):
        rows = rows_of(part)
        copies.append(
            pltpu.make_async_copy(vertex.at[0, 0, rows, :], u_out.at[rows, :], sems.at[2 + part])
        )
    for copy in copies:
        copy.start()
    copies[0].wait()
    copies[1].wait()
    c = c_in[...]
    ch, cl = halves(c)
    cc = jnp.concatenate([ch, cl], 0)
    total = jnp.zeros((CR, D), F32)
    for part in range(PARTS):
        rows = rows_of(part)
        copies[2 + part].wait()
        high, low = halves(u_out[rows, :])
        r = logit_gradient(ch, cc, high, low, tile[:, rows])
        r_out[:, rows] = r
        total = total + context_part(*halves(r), high, low)
    c_out[...] = c - lr_rate * total


def context_update(c, high_in, low_in, tile, c_out, r_out):
    ch, cl = halves(c)
    cc = jnp.concatenate([ch, cl], 0)
    total = jnp.zeros((CR, D), F32)
    for part in range(PARTS):
        rows = rows_of(part)
        high, low = high_in[rows, :], low_in[rows, :]
        r = logit_gradient(ch, cc, high, low, tile[:, rows])
        r_out[:, rows] = r
        total = total + context_part(*halves(r), high, low)
    c_out[...] = c - lr_rate * total


def is_odd():
    return lax.rem(lax.axis_index("blk"), 2) == 1


def odd_kernel(moved, high_in, low_in, tile, c_out, r_out, c_in, passed):
    del passed

    @pl.when(is_odd())
    def _():
        c = moved[...]
        c_in[...] = c
        context_update(c, high_in, low_in, tile, c_out, r_out)


def even_kernel(moved, high_in, low_in, tile, passed, r_old, c_old, c_out, r_out, c_in):
    del passed, r_old, c_old

    @pl.when(jnp.logical_not(is_odd()))
    def _():
        c = moved[...]
        c_in[...] = c
        context_update(c, high_in, low_in, tile, c_out, r_out)


def both_kernel(from_even, from_odd, high_in, low_in, tile, c_out, r_out, c_in):
    c = jnp.where(is_odd(), from_even[...], from_odd[...])
    c_in[...] = c
    context_update(c, high_in, low_in, tile, c_out, r_out)


def source_group(matching, group):
    source = jnp.int32(0)
    for k in range(N_GRP):
        source = jnp.where(matching[k] == group, jnp.int32(k), source)
    return source


def x_of(group):
    return (group // N_CORE) % N_X


def pack_kernel(matching, own, held, out):
    group = own[0]
    base = group - x_of(group) * N_CORE
    for x in range(N_X):
        source = source_group(matching, base + x * N_CORE)
        out[x] = held[(source // (N_X * N_CORE)) * N_CORE + source % N_CORE]


def received_update(matching, own, received, u_in, tile, c_out, r_out, c_in):
    c = received[x_of(source_group(matching, own[0]))]
    c_in[...] = c
    ch, cl = halves(c)
    cc = jnp.concatenate([ch, cl], 0)
    total = jnp.zeros((CR, D), F32)
    for part in range(PARTS):
        rows = rows_of(part)
        high, low = halves(u_in[rows, :])
        r = logit_gradient(ch, cc, high, low, tile[:, rows])
        r_out[:, rows] = r
        total = total + context_part(*halves(r), high, low)
    c_out[...] = c - lr_rate * total


def odd_received_kernel(*refs):
    *refs, passed = refs
    del passed

    @pl.when(is_odd())
    def _():
        received_update(*refs)


def even_received_kernel(matching, own, received, u_in, tile, passed, r_old, c_old, *outs):
    del passed, r_old, c_old

    @pl.when(jnp.logical_not(is_odd()))
    def _():
        received_update(matching, own, received, u_in, tile, *outs)


def gate_kernel(passed, out):
    del passed, out


def vertex_kernel(order, u_in, r_in, c_in, counts, u_out, tile, *rest, step):
    *halves_out, sem = rest
    copy = pltpu.make_async_copy(counts.at[0, 0, order[0, 0, step]], tile, sem)
    copy.start()
    ch, cl = halves(c_in[...])
    double = jnp.concatenate([ch, ch], 0)
    for part in range(PARTS):
        rows = rows_of(part)
        u = u_in[rows, :] - lr_rate * vertex_part(*halves(r_in[:, rows]), double, cl)
        u_out[rows, :] = u
        for half_out, half in zip(halves_out, halves(u)):
            half_out[rows, :] = half
    copy.wait()


def last_kernel(u_in, from_even, from_odd, high_in, low_in, tile, vertex_out, context_out, u_new, c_new, sems):
    c = jnp.where(is_odd(), from_even[...], from_odd[...])
    ch, cl = halves(c)
    cc = jnp.concatenate([ch, cl], 0)
    double = jnp.concatenate([ch, ch], 0)
    total = jnp.zeros((CR, D), F32)
    copies = []
    for part in range(PARTS):
        rows = rows_of(part)
        high, low = high_in[rows, :], low_in[rows, :]
        rh, rl = halves(logit_gradient(ch, cc, high, low, tile[:, rows]))
        u_new[rows, :] = u_in[rows, :] - lr_rate * vertex_part(rh, rl, double, cl)
        copies.append(
            pltpu.make_async_copy(u_new.at[rows, :], vertex_out.at[0, 0, rows, :], sems.at[part])
        )
        copies[-1].start()
        total = total + context_part(rh, rl, high, low)
    c_new[...] = c - lr_rate * total
    copies.append(pltpu.make_async_copy(c_new, context_out.at[0, 0], sems.at[PARTS]))
    copies[-1].start()
    for copy in copies:
        copy.wait()


MATMUL = 6 * CR * VR * D
BLOCK = 4 * CR * D
VERTEX = 4 * VR * D

UPDATED = (array((CR, D)), array((CR, VR)), array((CR, D)))


def first_step(order, vertex, context, counts):
    return call(
        first_kernel,
        UPDATED + (array((VR, D)),),
        [SMEM, HBM, HBM, HBM],
        (VMEM,) * 4,
        2 * MATMUL,
        2 * VERTEX,
        [pltpu.VMEM((CR, VR), jnp.int32), pltpu.SemaphoreType.DMA((2 + PARTS,))],
    )(order, vertex, context, counts)


PASSED = array((8, 128))


def gate(passed):
    return call(gate_kernel, PASSED, [VMEM], VMEM, 0, 8 * 128 * 4)(passed)


def odd_step(moved, high, low, tile):
    return call(
        odd_kernel, UPDATED + (PASSED,), [VMEM] * 4, (VMEM,) * 4, 2 * MATMUL, VERTEX
    )(moved, high, low, tile)


def even_step(moved, high, low, tile, passed, r, c):
    return call(
        even_kernel, UPDATED, [VMEM] * 7, (VMEM,) * 3, 2 * MATMUL, VERTEX, aliases={5: 1, 6: 2}
    )(moved, high, low, tile, passed, r, c)


def both_step(from_even, from_odd, high, low, tile):
    return call(
        both_kernel, UPDATED, [VMEM] * 5, (VMEM,) * 3, 2 * MATMUL, VERTEX
    )(from_even, from_odd, high, low, tile)


def odd_received_step(matching, own, received, u, tile):
    return call(
        odd_received_kernel,
        UPDATED + (PASSED,),
        [SMEM] * 2 + [VMEM] * 3,
        (VMEM,) * 4,
        2 * MATMUL,
        VERTEX,
    )(matching, own, received, u, tile)


def even_received_step(matching, own, received, u, tile, passed, r, c):
    return call(
        even_received_kernel,
        UPDATED,
        [SMEM] * 2 + [VMEM] * 6,
        (VMEM,) * 3,
        2 * MATMUL,
        VERTEX,
        aliases={6: 1, 7: 2},
    )(matching, own, received, u, tile, passed, r, c)


def vertex_step(order, u, r, c, counts, step):
    outs = (array((VR, D)), array((CR, VR), jnp.int32))
    if step != FIRST:
        outs += (array((VR, D), BF16),) * 2
    return call(
        functools.partial(vertex_kernel, step=step),
        outs,
        [SMEM, VMEM, VMEM, VMEM, HBM],
        (VMEM,) * len(outs),
        MATMUL,
        4 * VERTEX,
        [pltpu.SemaphoreType.DMA],
    )(order, u, r, c, counts)


def last_step(u, from_even, from_odd, high, low, tile):
    return call(
        last_kernel,
        (array((1, 1, VR, D)), array((1, 1, CR, D))),
        [VMEM] * 6,
        (HBM, HBM),
        3 * MATMUL,
        2 * VERTEX,
        [
            pltpu.VMEM((VR, D), F32),
            pltpu.VMEM((CR, D), F32),
            pltpu.SemaphoreType.DMA((PARTS + 1,)),
        ],
    )(u, from_even, from_odd, high, low, tile)


def pack(matching, own, held):
    return call(
        pack_kernel, array((N_X, CR, D)), [SMEM, SMEM, VMEM], VMEM, 0, 8 * BLOCK
    )(matching, own, held)


def shifted(block, parity):
    devices = lax.axis_size("blk")
    return lax.ppermute(block, "blk", [(i, (i + 1) % devices) for i in range(parity, devices, 2)])


def on_device(vertex, context, counts, tile_index, matching):
    own = lax.axis_index("grp").astype(jnp.int32).reshape(1)
    vertex, context, counts = (
        pltpu.with_memory_space_constraint(x, pltpu.HBM) for x in (vertex, context, counts)
    )
    half = N_X * N_CORE
    columns = [[g, g + 1, g + half, g + half + 1] for g in range(0, half, N_CORE)]
    rings = [[y * half + x * N_CORE + k for x in range(N_X)] for y in range(2) for k in range(N_CORE)]
    c_odd, r, c, u = first_step(tile_index, vertex, context, counts)
    c_even = c_odd
    for step in range(1, STEPS):
        if step == FIRST:
            held = lax.all_gather(c_odd, "grp", axis_index_groups=columns)
            sent = pack(matching, own, held)
            moved = lax.all_to_all(sent, "grp", 0, 0, axis_index_groups=rings, tiled=True)
        else:
            from_odd = shifted(c_odd, 1)
            from_even = shifted(c_even, 0)
        u, tile, *split = vertex_step(tile_index, u, r, c, counts, step)
        if step == STEPS - 1:
            return last_step(u, from_even, from_odd, *split, tile)
        if step == FIRST - 1:
            c_odd, r, c = both_step(from_even, from_odd, *split, tile)
            continue
        if step == FIRST:
            seen = (matching, own, moved, u, tile)
            odd, even, seen_even = odd_received_step, even_received_step, seen
        else:
            odd, even, seen, seen_even = odd_step, even_step, (from_even, *split, tile), (from_odd, *split, tile)
        c_odd, r, c, passed = odd(*seen)
        passed = gate(passed)
        c_even, r, c = even(*seen_even, passed, r, c)


def solution(mesh):
    in_specs = (
        P("grp", "blk", None, None),
        P("grp", "blk", None, None),
        P("grp", "blk", None, None, None),
        P("grp", "blk", None),
        P(),
    )
    out_specs = (P("grp", "blk", None, None), P("grp", "blk", None, None))
    return jax.shard_map(
        on_device, mesh=mesh, in_specs=in_specs, out_specs=out_specs, check_vma=False
    )
```

```python
import functools

import jax
import jax.numpy as jnp
from jax import lax
from jax.experimental import pallas as pl
from jax.experimental.pallas import tpu as pltpu
from jax.sharding import PartitionSpec as P

STEPS = 6
FIRST = 4
CR, VR, D = 96, 1024, 256
N_X, N_CORE = 4, 2
N_GRP = 16
lr_rate = 0.003

F32, BF16 = jnp.float32, jnp.bfloat16
CHUNK = 256
PARTS = VR // CHUNK
VMEM = pl.BlockSpec(memory_space=pltpu.VMEM)
SMEM = pl.BlockSpec(memory_space=pltpu.SMEM)
HBM = pl.BlockSpec(memory_space=pltpu.HBM)


def array(shape, dtype=F32):
    return jax.ShapeDtypeStruct(shape, dtype)


def call(kernel, out_shape, in_specs, out_specs, flops, moved, scratch=(), aliases=None):
    return pl.pallas_call(
        kernel,
        out_shape=out_shape,
        in_specs=in_specs,
        out_specs=out_specs,
        scratch_shapes=scratch,
        input_output_aliases=aliases or {},
        cost_estimate=pl.CostEstimate(flops=flops, bytes_accessed=moved, transcendentals=CR * VR),
        compiler_params=pltpu.CompilerParams(vmem_limit_bytes=16 * 1024 * 1024),
    )


def halves(x):
    high = x.astype(BF16)
    return high, (x - high.astype(F32)).astype(BF16)


def product(a, b, a_dim, b_dim):
    return lax.dot_general(a, b, (((a_dim,), (b_dim,)), ((), ())), preferred_element_type=F32)


def logits_of(ch, cc, high, low):
    both = product(cc, high, 1, 1)
    return both[:CR] + (both[CR:] + product(ch, low, 1, 1))


def gradient_of(logits, weight):
    weight = weight.astype(F32)
    return (weight + 1.0) * jax.nn.sigmoid(logits) - weight


def logit_gradient(ch, cc, high, low, weight):
    return gradient_of(logits_of(ch, cc, high, low), weight)


def context_part(rh, rl, high, low):
    both = product(jnp.concatenate([rh, rl], 0), high, 1, 0)
    return both[:CR] + (both[CR:] + product(rh, low, 1, 0))


def vertex_part(rh, rl, double, cl):
    return product(jnp.concatenate([rh, rl], 0), double, 0, 0) + product(rh, cl, 0, 0)


def rows_of(part):
    return pl.ds(part * CHUNK, CHUNK)


def first_kernel(
    order_hbm, vertex, context, counts, c_out, r_out, c_in, u_out, order, tile, highs, lows, sems
):
    order_copy = pltpu.make_async_copy(order_hbm.at[0, 0], order, sems.at[0])
    order_copy.start()
    c_copy = pltpu.make_async_copy(context.at[0, 0], c_in, sems.at[1])
    c_copy.start()
    u_copies = []
    for part in range(PARTS):
        rows = rows_of(part)
        u_copies.append(
            pltpu.make_async_copy(vertex.at[0, 0, rows, :], u_out.at[rows, :], sems.at[3 + part])
        )
        u_copies[-1].start()
    order_copy.wait()
    tile_copy = pltpu.make_async_copy(counts.at[0, 0, order[0]], tile, sems.at[2])
    tile_copy.start()
    c_copy.wait()
    c = c_in[...]
    ch, cl = halves(c)
    cc = jnp.concatenate([ch, cl], 0)
    for part in range(PARTS):
        rows = rows_of(part)
        u_copies[part].wait()
        high, low = halves(u_out[rows, :])
        highs[rows, :], lows[rows, :] = high, low
        r_out[:, rows] = logits_of(ch, cc, high, low)
    tile_copy.wait()
    total = jnp.zeros((CR, D), F32)
    for part in range(PARTS):
        rows = rows_of(part)
        r = gradient_of(r_out[:, rows], tile[:, rows])
        r_out[:, rows] = r
        total = total + context_part(*halves(r), highs[rows, :], lows[rows, :])
    c_out[...] = c - lr_rate * total


def context_update(c, high_in, low_in, tile, c_out, r_out):
    ch, cl = halves(c)
    cc = jnp.concatenate([ch, cl], 0)
    total = jnp.zeros((CR, D), F32)
    for part in range(PARTS):
        rows = rows_of(part)
        high, low = high_in[rows, :], low_in[rows, :]
        r = logit_gradient(ch, cc, high, low, tile[:, rows])
        r_out[:, rows] = r
        total = total + context_part(*halves(r), high, low)
    c_out[...] = c - lr_rate * total


def member(places):
    place = lax.rem(lax.axis_index("blk"), N_PLACES)
    return functools.reduce(jnp.logical_or, [place == p for p in places])


def take(blocks, targets, c_in):
    for block, places in zip(blocks, targets):

        @pl.when(member(places))
        def _(block=block):
            c_in[...] = block[...]


def context_kernel(*refs, places, targets, first):
    blocks, refs = refs[: len(targets)], refs[len(targets) :]
    high_in, low_in, tile = refs[:3]
    c_out, r_out, c_in = refs[3 if first else 5 :][:3]

    @pl.when(member(places))
    def _():
        take(blocks, targets, c_in)
        context_update(c_in[...], high_in, low_in, tile, c_out, r_out)


def source_group(matching, group):
    source = jnp.int32(0)
    for k in range(N_GRP):
        source = jnp.where(matching[k] == group, jnp.int32(k), source)
    return source


def x_of(group):
    return lax.rem(group // N_CORE, N_X)


def pack_kernel(matching, held, out, chosen, sems):
    group = lax.axis_index("grp")
    base = group - x_of(group) * N_CORE
    copies = []
    for x in range(N_X):
        source = source_group(matching, base + x * N_CORE)
        slot = (source // (N_X * N_CORE)) * N_CORE + lax.rem(source, N_CORE)
        copies.append(pltpu.make_async_copy(held.at[slot], out.at[x], sems.at[x]))
        copies[-1].start()
    chosen[...] = jnp.full(chosen.shape, x_of(source_group(matching, group)), jnp.int32)
    for copy in copies:
        copy.wait()


def received_kernel(*refs, places, first):
    chosen, received, u_in, tile = refs[:4]
    c_out, r_out, c_in = refs[4 if first else 7 :][:3]

    @pl.when(member(places))
    def _():
        from_x = chosen[0:1, 0:1]
        c = received[0]
        for x in range(1, N_X):
            c = jnp.where(from_x == x, received[x], c)
        c_in[...] = c
        ch, cl = halves(c)
        cc = jnp.concatenate([ch, cl], 0)
        total = jnp.zeros((CR, D), F32)
        for part in range(PARTS):
            rows = rows_of(part)
            high, low = halves(u_in[rows, :])
            r = logit_gradient(ch, cc, high, low, tile[:, rows])
            r_out[:, rows] = r
            total = total + context_part(*halves(r), high, low)
        c_out[...] = c - lr_rate * total


def gate_kernel(passed, out):
    del passed, out


def vertex_kernel(*refs, step, places, skipped, split):
    order, u_in, r_in, c_in, counts = refs[:5]
    u_out, tile, *halves_out, sem = refs[5 + skipped :]
    del split

    @pl.when(member(places))
    def _():
        lane = lax.broadcasted_iota(jnp.int32, (1, STEPS), 1)
        stored = jnp.max(jnp.where(lane == step, order[0], 0))
        copy = pltpu.make_async_copy(counts.at[0, 0, stored], tile, sem)
        copy.start()
        ch, cl = halves(c_in[...])
        double = jnp.concatenate([ch, ch], 0)
        for part in range(PARTS):
            rows = rows_of(part)
            u = u_in[rows, :] - lr_rate * vertex_part(*halves(r_in[:, rows]), double, cl)
            u_out[rows, :] = u
            for half_out, half in zip(halves_out, halves(u)):
                half_out[rows, :] = half
        copy.wait()


def last_kernel(*refs, targets):
    blocks, refs = refs[: len(targets)], refs[len(targets) :]
    u_in, high_in, low_in, tile, vertex_out, context_out, u_new, c_new, sems = refs
    take(blocks, targets, c_new)
    c = c_new[...]
    ch, cl = halves(c)
    cc = jnp.concatenate([ch, cl], 0)
    double = jnp.concatenate([ch, ch], 0)
    total = jnp.zeros((CR, D), F32)
    copies = []
    for part in range(PARTS):
        rows = rows_of(part)
        high, low = high_in[rows, :], low_in[rows, :]
        rh, rl = halves(logit_gradient(ch, cc, high, low, tile[:, rows]))
        u_new[rows, :] = u_in[rows, :] - lr_rate * vertex_part(rh, rl, double, cl)
        copies.append(
            pltpu.make_async_copy(u_new.at[rows, :], vertex_out.at[0, 0, rows, :], sems.at[part])
        )
        copies[-1].start()
        total = total + context_part(rh, rl, high, low)
    c_new[...] = c - lr_rate * total
    copies.append(pltpu.make_async_copy(c_new, context_out.at[0, 0], sems.at[PARTS]))
    copies[-1].start()
    for copy in copies:
        copy.wait()


MATMUL = 6 * CR * VR * D
BLOCK = 4 * CR * D
VERTEX = 4 * VR * D

UPDATED = (array((CR, D)), array((CR, VR)), array((CR, D)))


def first_step(order, vertex, context, counts):
    return call(
        first_kernel,
        UPDATED + (array((VR, D)),),
        [HBM] * 4,
        (VMEM,) * 4,
        2 * MATMUL,
        2 * VERTEX,
        [
            pltpu.SMEM((STEPS,), jnp.int32),
            pltpu.VMEM((CR, VR), jnp.int32),
            pltpu.VMEM((VR, D), BF16),
            pltpu.VMEM((VR, D), BF16),
            pltpu.SemaphoreType.DMA((3 + PARTS,)),
        ],
    )(order, vertex, context, counts)


PASSED = array((8, 128))


def gate(passed):
    return call(gate_kernel, PASSED, [VMEM], VMEM, 0, 8 * 128 * 4)(passed)


def context_step(places, blocks, targets, state, kept, last):
    first = not kept
    inputs = (*blocks, *state, *kept)
    at = len(blocks) + len(state)
    outs = UPDATED + (PASSED,) * (not last)
    return call(
        functools.partial(context_kernel, places=places, targets=targets, first=first),
        outs,
        [VMEM] * len(inputs),
        (VMEM,) * len(outs),
        2 * MATMUL,
        VERTEX,
        aliases=None if first else {at: 1, at + 1: 2},
    )(*inputs)


def received_step(places, chosen, received, u, tile, passed, kept, last):
    first = not kept
    inputs = (chosen, received, u, tile)
    if not first:
        inputs += (passed, *kept)
    outs = UPDATED + (PASSED,) * (not last)
    return call(
        functools.partial(received_kernel, places=places, first=first),
        outs,
        [VMEM] * len(inputs),
        (VMEM,) * len(outs),
        2 * MATMUL,
        VERTEX,
        aliases=None if first else {5: 1, 6: 2},
    )(*inputs)


def vertex_step(places, order, u, r, c, counts, step, passed, kept):
    split = step != FIRST
    outs = (array((VR, D)), array((CR, VR), jnp.int32)) + (array((VR, D), BF16),) * (2 * split)
    skipped = () if passed is None else (passed, *kept)
    aliases = {1: 0}
    if passed is not None:
        aliases.update({6 + k: 1 + k for k in range(len(kept))})
    return call(
        functools.partial(
            vertex_kernel, step=step, places=places, skipped=len(skipped), split=split
        ),
        outs,
        [VMEM, VMEM, VMEM, VMEM, HBM] + [VMEM] * len(skipped),
        (VMEM,) * len(outs),
        MATMUL,
        4 * VERTEX,
        [pltpu.SemaphoreType.DMA],
        aliases=aliases,
    )(order, u, r, c, counts, *skipped)


def last_step(u, high, low, tile, blocks, targets):
    return call(
        functools.partial(last_kernel, targets=targets),
        (array((1, 1, VR, D)), array((1, 1, CR, D))),
        [VMEM] * (4 + len(blocks)),
        (HBM, HBM),
        3 * MATMUL,
        2 * VERTEX,
        [
            pltpu.VMEM((VR, D), F32),
            pltpu.VMEM((CR, D), F32),
            pltpu.SemaphoreType.DMA((PARTS + 1,)),
        ],
    )(*blocks, u, high, low, tile)


def pack(matching, held):
    return call(
        pack_kernel,
        (array((N_X, CR, D)), array((8, 128), jnp.int32)),
        [SMEM, VMEM],
        (HBM, VMEM),
        0,
        8 * BLOCK,
        [pltpu.SemaphoreType.DMA((N_X,))],
    )(matching, held)


N_PLACES = 4
EVERY = (0, 1, 2, 3)
ORDER = {
    0: ((1, 2), (0, 3)),
    1: ((2,), (3,), (0, 1)),
    2: ((3,), (0, 1, 2)),
    3: (EVERY,),
    4: ((1, 2, 3), (0,)),
}


def shifted(block, places):
    devices = lax.axis_size("blk")
    route = [(i, (i + 1) % devices) for i in range(devices) if i % N_PLACES in places]
    return lax.ppermute(block, "blk", route)


def after(places):
    return {(p + 1) % N_PLACES for p in places}


def sources(places, step):
    served = [(k, sorted(after(group) & set(places))) for k, group in enumerate(ORDER[step - 1])]
    return [(k, tuple(group)) for k, group in served if group]


def on_device(vertex, context, counts, tile_index, matching):
    order = pltpu.with_memory_space_constraint(tile_index, pltpu.HBM)
    vertex, context, counts = (
        pltpu.with_memory_space_constraint(x, pltpu.HBM) for x in (vertex, context, counts)
    )
    half = N_X * N_CORE
    columns = [[g, g + 1, g + half, g + half + 1] for g in range(0, half, N_CORE)]
    rings = [[y * half + x * N_CORE + k for x in range(N_X)] for y in range(2) for k in range(N_CORE)]

    def send(block, step, k):
        return shifted(block, ORDER[step][k])

    c_new, r, c, u = first_step(order, vertex, context, counts)
    moved = [send(c_new, 0, k) for k in range(len(ORDER[0]))]
    for step in range(1, STEPS - 1):
        if step == FIRST:
            held = lax.all_gather(c_new, "grp", axis_index_groups=columns)
            sent, chosen = pack(matching, held)
            received = lax.all_to_all(sent, "grp", 0, 0, axis_index_groups=rings, tiled=True)
            u, tile = vertex_step(EVERY, tile_index, u, r, c, counts, step, None, ())
        new, passed, state, kept = [], None, (), ()
        for k, places in enumerate(ORDER[step]):
            if step != FIRST:
                u, *state = vertex_step(
                    places, tile_index, u, r, c, counts, step, passed, tuple(state)
                )
            last = k + 1 == len(ORDER[step])
            if step == FIRST:
                c_new, *kept = received_step(places, chosen, received, u, tile, passed, kept, last)
            else:
                tile, high, low = state
                wanted = sources(places, step)
                c_new, *kept = context_step(
                    places,
                    [moved[j] for j, _ in wanted],
                    [group for _, group in wanted],
                    (high, low, tile),
                    kept,
                    last,
                )
            if not last:
                *kept, passed = kept
            if step != FIRST - 1:
                new.append(send(c_new, step, k))
            if k + 1 < len(ORDER[step]):
                passed = gate(passed)
        moved = new
        r, c = kept
    step = STEPS - 1
    u, tile, high, low = vertex_step(EVERY, tile_index, u, r, c, counts, step, None, ())
    wanted = sources(EVERY, step)
    return last_step(u, high, low, tile, [moved[j] for j, _ in wanted], [g for _, g in wanted])


def solution(mesh):
    in_specs = (
        P("grp", "blk", None, None),
        P("grp", "blk", None, None),
        P("grp", "blk", None, None, None),
        P("grp", "blk", None),
        P(),
    )
    out_specs = (P("grp", "blk", None, None), P("grp", "blk", None, None))
    return jax.shard_map(
        on_device, mesh=mesh, in_specs=in_specs, out_specs=out_specs, check_vma=False
    )
```
